32 devices in a mesh: groups: 2 (over y), space: 4 (over z), tm: 2 (over x), rep: 2 (over core).
Axes of the slice: x: 2, y: 2, z: 4, core: 2. Of those that a mesh axis runs over, the one named last changes fastest.
Arguments:
- features: bfloat16 [1024, 16384], P(None, ('groups', 'space', 'tm', 'rep')), parts along dimension 1, may hold values from -6 to 6
- grad_out: bfloat16 [1024, 16384], P(None, ('groups', 'space', 'tm', 'rep')), parts along dimension 1, may hold values from -6 to 6
- query_weight: bfloat16 [1024, 1024], P('space'), may hold values from -0.1875 to 0.1875
- key_weight: bfloat16 [1024, 1024], P('space'), may hold values from -0.1875 to 0.1875
- value_weight: bfloat16 [1024, 1024], P('space'), may hold values from -0.1875 to 0.1875
- out_weight: bfloat16 [1024, 1024], P('space'), may hold values from -0.1875 to 0.1875
- query_scale: float32 [1024], replicated, may hold values from 0.1 to 1.9
- key_scale: float32 [1024], replicated, may hold values from 0.1 to 1.9
- value_scale: float32 [1024], replicated, may hold values from 0.1 to 1.9
- out_scale: float32 [1024], replicated, may hold values from 0.1 to 1.9
- active_blocks: int32 [32, 6], P(('groups', 'space', 'tm', 'rep')), parts along dimension 0, may hold values from 0 to 7, as said below
- active_count: int32 [32], P(('groups', 'space', 'tm', 'rep')), parts along dimension 0, may hold values from 1 to 6, as said below
Outputs:
- attention_out: bfloat16 [1024, 16384], P(None, ('groups', 'space', 'tm', 'rep')), parts along dimension 1
- input_grad: bfloat16 [1024, 16384], P(None, ('groups', 'space', 'tm', 'rep')), parts along dimension 1
The draws below stay inside these ranges and needn't reach their ends.
There are 2 independent parts, one for each index of `groups`. The reference program is written for one: setup_inputs(seed, part) draws one part's arguments, and reference() takes and returns one part's arrays. A program takes and returns all parts, laid end to end along the dimension named above; an argument that names none is the same for every part. Nothing has to cross between parts.
Inputs may be any that keep to these rules, and one draw needn't show every extreme that they name: `active_blocks`: each device's row holds 6 different block numbers of its 8 blocks. `active_count`: some device has all 6 listed blocks active in every draw.
All inputs are finite; a program needn't handle non-finite values.
Results may differ from the reference program's by a relative error of at most 0.0069.
Values may be sent and summed in bfloat16 or wider, within the bound.
No kernel may reach another device: no remote copies, remote signals or barrier semaphores. Data moves between devices by JAX's collectives and lax.ppermute only.
A program may use at most 64 MiB of HBM per device.

```python
import math
import jax
import jax.numpy as jnp
from jax import lax

HEADS = 16
HEAD_DIM = 64
D = 1024
BLOCK = 64
CAP = 6
BLK_DEV = 8
PLACES = 16
TOKENS = 8192
ROWS_ALL = 6144


def draw_active_blocks(key, part):
    place_keys = jax.random.split(jax.random.fold_in(key, 11), PLACES)
    orders = jax.vmap(lambda one_key: jax.random.permutation(one_key, BLK_DEV))(place_keys)
    return orders[:, :CAP].astype(jnp.int32)


def draw_active_count(key, part):
    counts = jax.random.randint(jax.random.fold_in(key, 21), (PLACES,), 1, CAP + 1)
    busiest = jax.random.randint(jax.random.fold_in(key, 22), (), 0, PLACES)
    return jnp.where(jnp.arange(PLACES) == busiest, CAP, counts).astype(jnp.int32)


def levels(own_key, dims, cuts, low, top_value):
    def one(position, blocks):
        heights = jax.random.uniform(jax.random.fold_in(jax.random.fold_in(own_key, 6), position), (blocks,), jnp.float32, low / len(cuts), top_value / len(cuts))
        return jnp.repeat(jnp.exp(heights), dims[position] // blocks).reshape((-1,) + (1,) * (len(dims) - position - 1))

    gain = one(*cuts[0])
    for cut in cuts[1:]:
        gain = gain * one(*cut)
    return gain


def gaussian(rng, dims, width, limit, pieces=(), held_as=jnp.bfloat16):
    drawn = width * jax.random.normal(rng, dims, jnp.float32)
    if pieces:
        drawn = drawn * levels(rng, dims, pieces, -0.22, 0.18)
    return jnp.clip(drawn, -limit, limit).astype(held_as)


def setup_inputs(seed: int = 0, part: int = 0) -> dict:
    streams_of = jax.random.split(jax.random.key(seed), 13)
    part_splits = jax.random.split(jax.random.fold_in(streams_of[12], part), 13)
    return {
        "features": gaussian(part_splits[0], (D, TOKENS), 1.0, 6.0, ((1, 16),)),
        "grad_out": gaussian(part_splits[1], (D, TOKENS), 1.0, 6.0, ((1, 16),)),
        "query_weight": gaussian(streams_of[2], (D, D), D ** -0.5, 0.1875, ((0, 4),)),
        "key_weight": gaussian(streams_of[3], (D, D), D ** -0.5, 0.1875, ((0, 4),)),
        "value_weight": gaussian(streams_of[4], (D, D), D ** -0.5, 0.1875, ((0, 4),)),
        "out_weight": gaussian(streams_of[5], (D, D), D ** -0.5, 0.1875, ((0, 4),)),
        "query_scale": jnp.clip(1.0 + 0.18 * jax.random.normal(streams_of[6], (D,), jnp.float32), 0.1, 1.9),
        "key_scale": jnp.clip(1.0 + 0.18 * jax.random.normal(streams_of[7], (D,), jnp.float32), 0.1, 1.9),
        "value_scale": jnp.clip(1.0 + 0.18 * jax.random.normal(streams_of[8], (D,), jnp.float32), 0.1, 1.9),
        "out_scale": jnp.clip(1.0 + 0.18 * jax.random.normal(streams_of[9], (D,), jnp.float32), 0.1, 1.9),
        "active_blocks": draw_active_blocks(jax.random.fold_in(jax.random.fold_in(streams_of[12], part), 71), part),
        "active_count": draw_active_count(jax.random.fold_in(jax.random.fold_in(streams_of[12], part), 71), part),
    }


highest = lax.Precision.HIGHEST

def compact_all(values, blocks, live_count):
    grid_view = values.reshape(values.shape[0], PLACES, BLK_DEV, BLOCK)
    places = jnp.arange(PLACES, dtype=jnp.int32)[:, None]
    picked = grid_view[:, places, blocks]
    live_mask = (jnp.arange(CAP, dtype=jnp.int32)[None, :] < live_count[:, None]).astype(values.dtype)
    picked = picked * live_mask[None, :, :, None]
    return picked.reshape(values.shape[0], PLACES * CAP * BLOCK)

def expand_all(values, blocks):
    places = jnp.arange(PLACES, dtype=jnp.int32)[:, None]
    shaped = values.reshape(values.shape[0], PLACES, CAP, BLOCK)
    target = jnp.zeros((values.shape[0], PLACES, BLK_DEV, BLOCK), values.dtype)
    return target.at[:, places, blocks].set(shaped).reshape(values.shape[0], TOKENS)

def to_heads(values):
    return values.reshape(HEADS, HEAD_DIM, -1).astype(jnp.float32)

def reference(features, grad_out, query_weight, key_weight, value_weight, out_weight, query_scale, key_scale, value_scale, out_scale, active_blocks, active_count):
    attn_scale = 1.0 / math.sqrt(HEAD_DIM * ROWS_ALL)
    scaled_grad = (grad_out.astype(jnp.float32) * out_scale[:, None]).astype(jnp.bfloat16)
    x_rows = compact_all(features, active_blocks, active_count)
    g_rows = compact_all(scaled_grad, active_blocks, active_count)
    query = (jnp.dot(query_weight.T, x_rows, preferred_element_type=jnp.float32) * query_scale[:, None]).astype(jnp.bfloat16)
    key = (jnp.dot(key_weight.T, x_rows, preferred_element_type=jnp.float32) * key_scale[:, None]).astype(jnp.bfloat16)
    value = (jnp.dot(value_weight.T, x_rows, preferred_element_type=jnp.float32) * value_scale[:, None]).astype(jnp.bfloat16)
    back = jnp.dot(out_weight, g_rows, preferred_element_type=jnp.float32).astype(jnp.bfloat16)
    q_heads = to_heads(query)
    k_heads = to_heads(key)
    v_heads = to_heads(value)
    b_heads = to_heads(back)
    state = jnp.einsum('hit,hjt->hij', k_heads, v_heads, precision=highest)
    state_grad = attn_scale * jnp.einsum('hit,hjt->hij', q_heads, b_heads, precision=highest)
    attended = (attn_scale * jnp.einsum('hij,hit->hjt', state, q_heads, precision=highest)).astype(jnp.bfloat16)
    attended = attended.reshape(D, -1)
    out_rows = (jnp.dot(out_weight.T, attended, preferred_element_type=jnp.float32) * out_scale[:, None]).astype(jnp.bfloat16)
    query_back = attn_scale * jnp.einsum('hij,hjt->hit', state, b_heads, precision=highest)
    query_back = (query_back.reshape(D, -1) * query_scale[:, None]).astype(jnp.bfloat16)
    key_back = jnp.einsum('hij,hjt->hit', state_grad, v_heads, precision=highest)
    key_back = (key_back.reshape(D, -1) * key_scale[:, None]).astype(jnp.bfloat16)
    value_back = jnp.einsum('hij,hit->hjt', state_grad, k_heads, precision=highest)
    value_back = (value_back.reshape(D, -1) * value_scale[:, None]).astype(jnp.bfloat16)
    in_rows = jnp.dot(query_weight, query_back, preferred_element_type=jnp.float32)
    in_rows = in_rows + jnp.dot(key_weight, key_back, preferred_element_type=jnp.float32)
    in_rows = in_rows + jnp.dot(value_weight, value_back, preferred_element_type=jnp.float32)
    in_rows = in_rows.astype(jnp.bfloat16)
    return (expand_all(out_rows, active_blocks), expand_all(in_rows, active_blocks))
```

```python
import functools
import math

import jax
import jax.numpy as jnp
from jax import lax
from jax.experimental import pallas as pl
from jax.experimental.pallas import tpu as pltpu
from jax.sharding import PartitionSpec as P

HEADS = 16
HEAD_DIM = 64
BLOCK = 64
BF16 = jnp.bfloat16
F32 = jnp.float32
REDUCE_AXES = ("space", "tm", "rep")
DEVICE_AXES = ("groups", "space", "tm", "rep")

VMEM = pl.BlockSpec(memory_space=pltpu.VMEM)
ANY = pl.BlockSpec(memory_space=pl.ANY)
SMEM = pl.BlockSpec(memory_space=pltpu.SMEM)


def dot(a, b, ca, cb):
    return lax.dot_general(a, b, (((ca,), (cb,)), ((), ())), preferred_element_type=F32)


def call(body, outs, in_specs, args, scratch=(), flops=0, limit=None):
    size = sum(math.prod(o.shape) * o.dtype.itemsize for o in outs)
    size += sum(math.prod(a.shape) * a.dtype.itemsize for a in args)
    return pl.pallas_call(
        body,
        out_shape=tuple(outs),
        in_specs=in_specs,
        out_specs=(VMEM,) * len(outs),
        scratch_shapes=scratch,
        compiler_params=pltpu.CompilerParams(vmem_limit_bytes=limit),
        cost_estimate=pl.CostEstimate(flops=flops, bytes_accessed=size, transcendentals=0),
    )(*args)


def shape(dims, dtype=BF16):
    return jax.ShapeDtypeStruct(dims, dtype)


def swap_x(a):
    return lax.ppermute(a, "tm", [(0, 1), (1, 0)])


def swap_y(a):
    return lax.ppermute(a, "groups", [(0, 1), (1, 0)])


def swap_core(a):
    return lax.ppermute(a, "rep", [(0, 1), (1, 0)])


def turn_z(a, step):
    return lax.ppermute(a, "space", [(i, (i + step) % 4) for i in range(4)])


def swap_z(a, bit):
    return lax.ppermute(a, "space", [(i, i ^ bit) for i in range(4)])


def cat(*parts):
    return jnp.concatenate(parts, 0)


def around(piece):
    return cat(turn_z(piece, 1), turn_z(piece, 3), turn_z(piece, 2))


def spread(mine, first, second):
    pair = cat(mine, first(mine))
    return pair, second(pair)


def sum_over_chips(part):
    for swap in (swap_x, lambda a: swap_z(a, 1), lambda a: swap_z(a, 2)):
        part = part + swap(part.astype(BF16)).astype(F32)
    return part


def place(pos_ref, own_ref, pair_ref, far_ref, full_ref, sems, flips, base):
    z, q = pos_ref[0], pos_ref[1]
    rows = pair_ref.shape[0] // 6
    whole = own_ref.shape[0]
    copies = [
        pltpu.make_async_copy(
            own_ref, full_ref.at[pl.ds(pl.multiple_of(z * whole, whole), whole)], sems.at[base]
        )
    ]
    order = ((pair_ref, 0), (pair_ref, flips[0]), (far_ref, flips[1]), (far_ref, 3))
    for n, (ref, flip) in enumerate(order):
        for k, step in enumerate((3, 1, 2)):
            at = lax.rem(z + step, 4) * 4 + lax.bitwise_xor(q, flip)
            copies.append(
                pltpu.make_async_copy(
                    ref.at[pl.ds((3 * (n % 2) + k) * rows, rows)],
                    full_ref.at[pl.ds(pl.multiple_of(at * rows, rows), rows)],
                    sems.at[base + 1 + 3 * n + k],
                )
            )
    return copies


def pack(block):
    left = lax.broadcasted_iota(jnp.int32, (HEAD_DIM, 128), 1) < HEAD_DIM
    return (
        jnp.where(left, block[0:64, 0:128], block[64:128, 0:128]),
        jnp.where(left, block[128:192, 128:256], block[192:256, 128:256]),
    )


def unpack(packed, full_ref):
    left = lax.broadcasted_iota(jnp.int32, (HEAD_DIM, 128), 1) < HEAD_DIM
    full_ref[...] = jnp.zeros_like(full_ref)
    for n in range(2):
        two = packed[64 * n : 64 * n + 64]
        full_ref[128 * n : 128 * n + 64, 128 * n : 128 * n + 128] = jnp.where(
            left, two, 0.0
        ).astype(full_ref.dtype)
        full_ref[128 * n + 64 : 128 * n + 128, 128 * n : 128 * n + 128] = jnp.where(
            left, 0.0, two
        ).astype(full_ref.dtype)


def key_value_body(
    pos, x_own, x_other, ko, kp, kf, vo, vp, vf, ks, vs, key, value, state, wk, wv, sems
):
    copies = place(pos, ko, kp, kf, wk, sems, (1, 2), 0)
    copies += place(pos, vo, vp, vf, wv, sems, (2, 1), 13)
    for one in copies:
        one.start()
    for one in copies:
        one.wait()
    half = x_own.shape[0]
    for n, rows in enumerate((x_own, x_other)):
        for t in range(0, half, 256):
            tile = rows[t : t + 256, :]
            at = slice(n * half + t, n * half + t + 256)
            key[at, :] = (dot(tile, wk[...], 1, 0) * ks[...]).astype(BF16)
            value[at, :] = (dot(tile, wv[...], 1, 0) * vs[...]).astype(BF16)
    for g in range(2):
        cols = slice(256 * g, 256 * g + 256)
        a, b = pack(dot(key[:, cols], value[:, cols], 0, 0))
        state[128 * g : 128 * g + 64, :] = a
        state[128 * g + 64 : 128 * g + 128, :] = b


def query_back_body(
    scale, pos, x_own, x_other, g_own, g_other, qo, qp, qf, oo, op, of, qs,
    query, back, term, wq, wo, sems,
):
    copies = place(pos, qo, qp, qf, wq, sems, (1, 2), 0)
    copies += place(pos, oo, op, of, wo, sems, (2, 1), 13)
    for one in copies:
        one.start()
    for one in copies:
        one.wait()
    half = x_own.shape[0]
    for n, rows in enumerate((x_own, x_other)):
        for t in range(0, half, 256):
            at = slice(n * half + t, n * half + t + 256)
            query[at, :] = (dot(rows[t : t + 256, :], wq[...], 1, 0) * qs[...]).astype(BF16)
    for n, cols in enumerate((g_own, g_other)):
        for t in range(0, half, 256):
            at = slice(n * half + t, n * half + t + 256)
            back[:, at] = dot(wo[...], cols[:, t : t + 256], 1, 0).astype(BF16)
    for g in range(2):
        part = slice(256 * g, 256 * g + 256)
        a, b = pack(scale * dot(back[part, :], query[:, part], 1, 0))
        term[128 * g : 128 * g + 64, :] = a
        term[128 * g + 64 : 128 * g + 128, :] = b


def middle_body(
    scale, query, back, state, wq, wo, qs, out_own, out_other, in_own, in_other, diag, att, qb
):
    half = out_own.shape[0]
    for g in range(2):
        part = slice(256 * g, 256 * g + 256)
        unpack(scale * state[128 * g : 128 * g + 128, :], diag)
        att[:, part] = dot(query[:, part], diag[...], 1, 0).astype(BF16)
        qb[part, :] = (dot(diag[...], back[part, :], 1, 0) * qs[part, :]).astype(BF16)
    for n, (out, inp) in enumerate(((out_own, in_own), (out_other, in_other))):
        for t in range(0, half, 256):
            at = slice(n * half + t, n * half + t + 256)
            out[t : t + 256, :] = dot(att[at, :], wo[...], 1, 0).astype(out.dtype)
            inp[:, t : t + 256] = dot(wq[...], qb[:, at], 1, 0)


def tail_body(key, value, term, wk, wv, ks, vs, in_own, in_other, res_own, res_other, diag, kb, vb):
    half = in_own.shape[1]
    for g in range(2):
        part = slice(256 * g, 256 * g + 256)
        unpack(term[128 * g : 128 * g + 128, :], diag)
        kb[:, part] = (dot(value[:, part], diag[...], 1, 0) * ks[:, part]).astype(BF16)
        vb[:, part] = (dot(key[:, part], diag[...], 1, 1) * vs[:, part]).astype(BF16)
    for n, (inp, res) in enumerate(((in_own, res_own), (in_other, res_other))):
        for t in range(0, half, 256):
            at = slice(n * half + t, n * half + t + 256)
            total = inp[:, t : t + 256] + dot(wk[...], kb[at, :], 1, 1)
            total = total + dot(wv[...], vb[at, :], 1, 1)
            res[:, t : t + 256] = total.astype(res.dtype)


def per_device_split(
    features,
    grad_out,
    query_weight,
    key_weight,
    value_weight,
    out_weight,
    query_scale,
    key_scale,
    value_scale,
    out_scale,
    active_blocks,
    active_count,
):
    x, y, z, c = (lax.axis_index(a) for a in ("tm", "groups", "space", "rep"))
    width, tokens = features.shape
    mine = width // 2
    both = 2 * tokens
    quarter = 2 * y + x
    slots = active_blocks.shape[1] * BLOCK
    scale = 1.0 / math.sqrt(HEAD_DIM * slots * lax.axis_size(REDUCE_AXES))
    pos = jnp.stack([z, quarter]).astype(jnp.int32)

    def columns(shard):
        split = shard.reshape(shard.shape[0], 4, 2, 128)
        return lax.dynamic_index_in_dim(split, c, 2, keepdims=False).reshape(-1, mine)

    def own_piece(own):
        rows = own.shape[0] // 4
        return lax.dynamic_slice_in_dim(own, quarter * rows, rows, 0)

    def own_scale(v):
        return lax.dynamic_index_in_dim(v.reshape(4, 2, 128), c, 1, keepdims=False).reshape(mine)

    k_own, v_own, q_own = columns(key_weight), columns(value_weight), columns(query_weight)
    o_own = lax.dynamic_slice_in_dim(out_weight, c * 128, 128, 0)
    k_pair, k_far = spread(around(own_piece(k_own)), swap_x, swap_y)
    v_pair, v_far = spread(around(own_piece(v_own)), swap_y, swap_x)
    q_pair, q_far = spread(around(own_piece(q_own)), swap_x, swap_y)
    o_pair, o_far = spread(around(own_piece(o_own)), swap_y, swap_x)

    live = jnp.arange(active_blocks.shape[1], dtype=jnp.int32) < active_count[0]
    named = jnp.where(live, active_blocks[0], -1)
    block_of = jnp.arange(tokens, dtype=jnp.int32) // BLOCK
    mask = jnp.any(named[:, None] == block_of[None, :], axis=0)
    zero = jnp.zeros((), BF16)
    x_own = jnp.where(mask[:, None], features.T, zero)
    g_own = (grad_out.astype(F32) * out_scale[:, None]).astype(BF16)
    g_own = jnp.where(mask[None, :], g_own, zero)
    x_other, g_other = swap_core(x_own), swap_core(g_own)

    ks, vs, qs = own_scale(key_scale), own_scale(value_scale), own_scale(query_scale)
    sems = (pltpu.SemaphoreType.DMA((26,)),)
    ff = 2 * both * width * mine
    key, value, state, wk, wv = call(
        key_value_body,
        [shape((both, mine)), shape((both, mine)), shape((256, 128), F32),
         shape((width, mine)), shape((width, mine))],
        [SMEM, VMEM, VMEM] + [ANY] * 6 + [VMEM] * 2,
        (pos, x_own, x_other, k_own, k_pair, k_far, v_own, v_pair, v_far, ks[None], vs[None]),
        sems, 2 * ff, 24 << 20,
    )
    state = sum_over_chips(state)
    query, back, term, wq, wo = call(
        functools.partial(query_back_body, scale),
        [shape((both, mine)), shape((mine, both)), shape((256, 128), F32),
         shape((width, mine)), shape((mine, width))],
        [SMEM] + [VMEM] * 4 + [ANY] * 6 + [VMEM],
        (pos, x_own, x_other, g_own, g_other, q_own, q_pair, q_far, o_own, o_pair, o_far, qs[None]),
        sems, 2 * ff, 24 << 20,
    )
    term = sum_over_chips(term)
    diag = pltpu.VMEM((256, 256), BF16)
    out_own, out_other, in_own, in_other = call(
        functools.partial(middle_body, scale),
        [shape((tokens, width), F32), shape((tokens, width)),
         shape((width, tokens), F32), shape((width, tokens), F32)],
        [VMEM] * 6,
        (query, back, state, wq, wo, qs[:, None]),
        (diag, pltpu.VMEM((both, mine), BF16), pltpu.VMEM((mine, both), BF16)),
        2 * ff, 32 << 20,
    )
    out_sum = out_own + swap_core(out_other).astype(F32)
    attention_out = (out_sum * out_scale[None, :]).astype(BF16).T
    res_own, res_other = call(
        tail_body,
        [shape((width, tokens), F32), shape((width, tokens))],
        [VMEM] * 9,
        (key, value, term, wk, wv, ks[None], vs[None], in_own, in_other),
        (diag, pltpu.VMEM((both, mine), BF16), pltpu.VMEM((both, mine), BF16)),
        2 * ff, 32 << 20,
    )
    input_grad = (res_own + swap_core(res_other).astype(F32)).astype(BF16)
    return attention_out, input_grad


highest = lax.Precision.HIGHEST
contract_first = (((0,), (0,)), ((), ()))


def compact_local(values, blocks, live_count):
    feature_rows = values.shape[0]
    block_grid = values.reshape(feature_rows, -1, BLOCK)
    picked = jnp.take(block_grid, blocks, axis=1)
    live_mask = (jnp.arange(blocks.shape[0], dtype=jnp.int32) < live_count).astype(values.dtype)
    return (picked * live_mask[None, :, None]).reshape(feature_rows, blocks.shape[0] * BLOCK)


def expand_local(values, blocks, total_blocks):
    feature_rows = values.shape[0]
    shaped = values.reshape(feature_rows, blocks.shape[0], BLOCK)
    target = jnp.zeros((feature_rows, total_blocks, BLOCK), values.dtype)
    return target.at[:, blocks, :].set(shaped).reshape(feature_rows, total_blocks * BLOCK)


def per_device_whole(
    features,
    grad_out,
    query_weight,
    key_weight,
    value_weight,
    out_weight,
    query_scale,
    key_scale,
    value_scale,
    out_scale,
    active_blocks,
    active_count,
):
    blocks = active_blocks[0]
    live_count = active_count[0]
    total_blocks = features.shape[1] // BLOCK
    slot_rows = blocks.shape[0] * BLOCK
    model_width = features.shape[0]
    attn_scale = 1.0 / math.sqrt(HEAD_DIM * slot_rows * lax.axis_size(("space", "tm", "rep")))
    scaled_grad = (grad_out.astype(jnp.float32) * out_scale[:, None]).astype(jnp.bfloat16)
    x_rows = compact_local(features, blocks, live_count)
    g_rows = compact_local(scaled_grad, blocks, live_count)
    pieces = (
        lax.all_gather(query_weight, "space", axis=0, tiled=True),
        lax.all_gather(key_weight, "space", axis=0, tiled=True),
        lax.all_gather(value_weight, "space", axis=0, tiled=True),
    )
    part_rows = x_rows
    q_raw, k_raw, v_raw = tuple(
        (
            lax.dot_general(piece_w, part_rows, contract_first, preferred_element_type=jnp.float32)
            for piece_w in pieces
        )
    )
    back_raw = jnp.dot(
        lax.all_gather(out_weight, "space", axis=0, tiled=True),
        g_rows,
        preferred_element_type=jnp.float32,
    )
    query = (q_raw * query_scale[:, None]).astype(jnp.bfloat16)
    key = (k_raw * key_scale[:, None]).astype(jnp.bfloat16)
    value = (v_raw * value_scale[:, None]).astype(jnp.bfloat16)
    back = back_raw.astype(jnp.bfloat16)
    q_heads = query.reshape(HEADS, HEAD_DIM, slot_rows)
    k_heads = key.reshape(HEADS, HEAD_DIM, slot_rows)
    v_heads = value.reshape(HEADS, HEAD_DIM, slot_rows)
    b_heads = back.reshape(HEADS, HEAD_DIM, slot_rows)
    state_local = jnp.einsum("hit,hjt->hij", k_heads, v_heads, preferred_element_type=jnp.float32)
    grad_local = attn_scale * jnp.einsum(
        "hit,hjt->hij", q_heads, b_heads, preferred_element_type=jnp.float32
    )
    state, state_grad = lax.psum((state_local, grad_local), ("space", "tm", "rep"))
    attended = attn_scale * jnp.einsum(
        "hij,hit->hjt", state, q_heads.astype(jnp.float32), precision=highest
    )
    attended = attended.astype(jnp.bfloat16).reshape(model_width, slot_rows)
    query_back = attn_scale * jnp.einsum(
        "hij,hjt->hit", state, b_heads.astype(jnp.float32), precision=highest
    )
    query_back = (query_back.reshape(model_width, slot_rows) * query_scale[:, None]).astype(
        jnp.bfloat16
    )
    key_back = jnp.einsum(
        "hij,hjt->hit", state_grad, v_heads.astype(jnp.float32), precision=highest
    )
    key_back = (key_back.reshape(model_width, slot_rows) * key_scale[:, None]).astype(jnp.bfloat16)
    value_back = jnp.einsum(
        "hij,hit->hjt", state_grad, k_heads.astype(jnp.float32), precision=highest
    )
    value_back = (value_back.reshape(model_width, slot_rows) * value_scale[:, None]).astype(
        jnp.bfloat16
    )
    part_rows = attended
    y_raw = lax.dot_general(
        lax.all_gather(out_weight, "space", axis=0, tiled=True),
        part_rows,
        contract_first,
        preferred_element_type=jnp.float32,
    )
    pieces = (
        lax.all_gather(query_weight, "space", axis=0, tiled=True),
        lax.all_gather(key_weight, "space", axis=0, tiled=True),
        lax.all_gather(value_weight, "space", axis=0, tiled=True),
    )
    new_rows = jnp.dot(pieces[0], query_back, preferred_element_type=jnp.float32)
    new_rows = new_rows + jnp.dot(pieces[1], key_back, preferred_element_type=jnp.float32)
    new_rows = new_rows + jnp.dot(pieces[2], value_back, preferred_element_type=jnp.float32)
    out_rows = (y_raw * out_scale[:, None]).astype(jnp.bfloat16)
    in_rows = new_rows.astype(jnp.bfloat16)
    return (
        expand_local(out_rows, blocks, total_blocks),
        expand_local(in_rows, blocks, total_blocks),
    )


def solution(mesh):
    fits = mesh.shape["space"] == 4 and all(
        mesh.shape[a] == 2 for a in ("groups", "tm", "rep")
    )
    split = P(None, DEVICE_AXES)
    placed = (
        split,
        split,
        P("space", None),
        P("space", None),
        P("space", None),
        P("space", None),
        P(),
        P(),
        P(),
        P(),
        P(DEVICE_AXES, None),
        P(DEVICE_AXES),
    )
    return jax.shard_map(
        per_device_split if fits else per_device_whole,
        mesh=mesh,
        in_specs=placed,
        out_specs=(split, split),
        check_vma=False,
    )
```

```python
import functools
import math

import jax
import jax.numpy as jnp
from jax import lax
from jax.experimental import pallas as pl
from jax.experimental.pallas import tpu as pltpu
from jax.sharding import PartitionSpec as P

HEADS = 16
HEAD_DIM = 64
BLOCK = 64
BF16 = jnp.bfloat16
F32 = jnp.float32
REDUCE_AXES = ("space", "tm", "rep")
DEVICE_AXES = ("groups", "space", "tm", "rep")

VMEM = pl.BlockSpec(memory_space=pltpu.VMEM)
ANY = pl.BlockSpec(memory_space=pl.ANY)
SMEM = pl.BlockSpec(memory_space=pltpu.SMEM)


def dot(a, b, ca, cb):
    return lax.dot_general(a, b, (((ca,), (cb,)), ((), ())), preferred_element_type=F32)


def call(body, outs, in_specs, args, scratch=(), flops=0, limit=None, out_specs=None):
    size = sum(math.prod(o.shape) * o.dtype.itemsize for o in outs)
    size += sum(math.prod(a.shape) * a.dtype.itemsize for a in args)
    return pl.pallas_call(
        body,
        out_shape=tuple(outs),
        in_specs=in_specs,
        out_specs=out_specs or (VMEM,) * len(outs),
        scratch_shapes=scratch,
        compiler_params=pltpu.CompilerParams(vmem_limit_bytes=limit),
        cost_estimate=pl.CostEstimate(flops=flops, bytes_accessed=size, transcendentals=0),
    )(*args)


def shape(dims, dtype=BF16):
    return jax.ShapeDtypeStruct(dims, dtype)


def swap_x(a):
    return lax.ppermute(a, "tm", [(0, 1), (1, 0)])


def swap_y(a):
    return lax.ppermute(a, "groups", [(0, 1), (1, 0)])


def swap_core(a):
    return lax.ppermute(a, "rep", [(0, 1), (1, 0)])


def turn_z(a, step):
    return lax.ppermute(a, "space", [(i, (i + step) % 4) for i in range(4)])


def pieces(half, swap):
    near = tuple(turn_z(half, step) for step in (1, 3, 2))
    return near + tuple(swap(a) for a in near)


def sum_over_chips(part):
    part = part + swap_x(part.astype(BF16)).astype(F32)
    sent = part.astype(BF16)
    for step in (1, 3, 2):
        part = part + turn_z(sent, step).astype(F32)
    return part


def aligned(index, size):
    return pl.ds(pl.multiple_of(index * size, size), size)


def send_body(pos, q, k, v, o, q_half, k_half, v_half, o_half, sems):
    c, x, y = pos[1], pos[2], pos[3]
    copies = []
    for n, (ref, half, bit) in enumerate(((q, q_half, x), (k, k_half, x), (v, v_half, y))):
        for j in range(4):
            cols = pl.ds(pl.multiple_of(256 * j + 128 * c, 128), 128)
            copies.append(
                pltpu.make_async_copy(
                    ref.at[aligned(bit, half.shape[0]), cols],
                    half.at[:, 128 * j : 128 * j + 128],
                    sems.at[4 * n + j],
                )
            )
    copies.append(
        pltpu.make_async_copy(o.at[aligned(2 * c + y, o_half.shape[0])], o_half, sems.at[12])
    )
    for one in copies:
        one.start()
    for one in copies:
        one.wait()


def mask_body(blocks, count, features, grad, scale, rows, cols):
    tokens = features.shape[1]
    block_of = lax.broadcasted_iota(jnp.int32, (1, tokens), 1) // BLOCK
    mask = jnp.zeros((1, tokens), F32)
    for j in range(blocks.shape[1]):
        named = jnp.where(j < count[0], blocks[0, j], -1)
        mask = jnp.where(block_of == named, 1.0, mask)
    for t in range(0, features.shape[0], 256):
        at = slice(t, t + 256)
        rows[:, at] = (features[at, :].astype(F32) * mask).astype(BF16).T
        cols[at, :] = (grad[at, :].astype(F32) * scale[at, :] * mask).astype(BF16)


def place(pos_ref, own_ref, parts, full_ref, sems, axis, base, by_rows=False):
    z, c, bit = pos_ref[0], pos_ref[1], pos_ref[axis]
    rows = parts[0].shape[0]
    whole = 2 * rows
    copies = []

    def add(src, dst):
        copies.append(pltpu.make_async_copy(src, dst, sems.at[base + len(copies)]))

    if by_rows:
        add(own_ref.at[aligned(c, whole)], full_ref.at[aligned(z, whole)])
    else:
        for j in range(4):
            cols = pl.ds(pl.multiple_of(256 * j + 128 * c, 128), 128)
            add(own_ref.at[:, cols], full_ref.at[aligned(z, whole), 128 * j : 128 * j + 128])
    for n, ref in enumerate(parts):
        at = lax.rem(z + (3, 1, 2)[n % 3], 4) * 2 + (bit if n < 3 else 1 - bit)
        add(ref, full_ref.at[aligned(at, rows)])
    for one in copies:
        one.start()
    return copies


def wait(copies):
    for one in copies:
        one.wait()


def pack(block):
    left = lax.broadcasted_iota(jnp.int32, (HEAD_DIM, 128), 1) < HEAD_DIM
    return (
        jnp.where(left, block[0:64, 0:128], block[64:128, 0:128]),
        jnp.where(left, block[128:192, 128:256], block[192:256, 128:256]),
    )


def unpack(packed, full_ref):
    left = lax.broadcasted_iota(jnp.int32, (HEAD_DIM, 128), 1) < HEAD_DIM
    full_ref[...] = jnp.zeros_like(full_ref)
    for n in range(2):
        two = packed[64 * n : 64 * n + 64]
        full_ref[128 * n : 128 * n + 64, 128 * n : 128 * n + 128] = jnp.where(
            left, two, 0.0
        ).astype(full_ref.dtype)
        full_ref[128 * n + 64 : 128 * n + 128, 128 * n : 128 * n + 128] = jnp.where(
            left, 0.0, two
        ).astype(full_ref.dtype)


def key_value_body(pos, x_own, x_other, ks, vs, *refs):
    k, v = refs[0:7], refs[7:14]
    key_out, value_out, state, key, value, wk, wv, sems = refs[14:]
    fetch_k = place(pos, k[0], k[1:], wk, sems, 2, 0)
    fetch_v = place(pos, v[0], v[1:], wv, sems, 3, 10)
    half = x_own.shape[0]
    stores = []
    for fetch, w, scale, dst, out in (
        (fetch_k, wk, ks, key, key_out), (fetch_v, wv, vs, value, value_out)
    ):
        wait(fetch)
        for n, rows in enumerate((x_own, x_other)):
            for t in range(0, half, 256):
                at = slice(n * half + t, n * half + t + 256)
                dst[at, :] = (dot(rows[t : t + 256, :], w[...], 1, 0) * scale[...]).astype(BF16)
        stores.append(pltpu.make_async_copy(dst, out, sems.at[20 + len(stores)]))
        stores[-1].start()
    for g in range(2):
        cols = slice(256 * g, 256 * g + 256)
        a, b = pack(dot(key[:, cols], value[:, cols], 0, 0))
        state[128 * g : 128 * g + 64, :] = a
        state[128 * g + 64 : 128 * g + 128, :] = b
    wait(stores)


def query_back_body(scale, pos, x_own, x_other, g_own, g_other, qs, *refs):
    q, o = refs[0:7], refs[7:14]
    query, back, term, wq, wo, sems = refs[14:]
    fetch_q = place(pos, q[0], q[1:], wq, sems, 2, 0)
    fetch_o = place(pos, o[0], o[1:], wo, sems, 3, 10, True)
    half = x_own.shape[0]
    wait(fetch_q)
    for n, rows in enumerate((x_own, x_other)):
        for t in range(0, half, 256):
            at = slice(n * half + t, n * half + t + 256)
            query[at, :] = (dot(rows[t : t + 256, :], wq[...], 1, 0) * qs[...]).astype(BF16)
    wait(fetch_o)
    for n, cols in enumerate((g_own, g_other)):
        for t in range(0, half, 256):
            at = slice(n * half + t, n * half + t + 256)
            back[:, at] = dot(wo[...], cols[:, t : t + 256], 1, 0).astype(BF16)
    for g in range(2):
        part = slice(256 * g, 256 * g + 256)
        a, b = pack(scale * dot(back[part, :], query[:, part], 1, 0))
        term[128 * g : 128 * g + 64, :] = a
        term[128 * g + 64 : 128 * g + 128, :] = b


def middle_body(scale, pos, query, back, state, qs, *refs):
    q, o = refs[0:7], refs[7:14]
    out_own, out_other, in_own, in_other, diag, att, qb, wq, wo, sems = refs[14:]
    fetch_o = place(pos, o[0], o[1:], wo, sems, 3, 10, True)
    fetch_q = place(pos, q[0], q[1:], wq, sems, 2, 0)
    half = out_own.shape[0]
    for g in range(2):
        part = slice(256 * g, 256 * g + 256)
        unpack(scale * state[128 * g : 128 * g + 128, :], diag)
        att[:, part] = dot(query[:, part], diag[...], 1, 0).astype(BF16)
        qb[part, :] = (dot(diag[...], back[part, :], 1, 0) * qs[part, :]).astype(BF16)
    wait(fetch_o)
    wait(fetch_q)
    for n, (out, inp) in enumerate(((out_own, in_own), (out_other, in_other))):
        for t in range(0, half, 256):
            at = slice(n * half + t, n * half + t + 256)
            out[t : t + 256, :] = dot(att[at, :], wo[...], 1, 0).astype(out.dtype)
            inp[:, t : t + 256] = dot(wq[...], qb[:, at], 1, 0)


def tail_body(pos, key, value, term, ks, vs, in_own, in_other, *refs):
    k, v = refs[0:7], refs[7:14]
    res_own, res_other, diag, kb, vb, wk, wv, sems = refs[14:]
    fetch = place(pos, k[0], k[1:], wk, sems, 2, 0)
    fetch += place(pos, v[0], v[1:], wv, sems, 3, 10)
    half = in_own.shape[1]
    for g in range(2):
        part = slice(256 * g, 256 * g + 256)
        unpack(term[128 * g : 128 * g + 128, :], diag)
        kb[:, part] = (dot(value[:, part], diag[...], 1, 0) * ks[:, part]).astype(BF16)
        vb[:, part] = (dot(key[:, part], diag[...], 1, 1) * vs[:, part]).astype(BF16)
    wait(fetch)
    for n, (inp, res) in enumerate(((in_own, res_own), (in_other, res_other))):
        for t in range(0, half, 256):
            at = slice(n * half + t, n * half + t + 256)
            total = inp[:, t : t + 256] + dot(wk[...], kb[at, :], 1, 1)
            total = total + dot(wv[...], vb[at, :], 1, 1)
            res[:, t : t + 256] = total.astype(res.dtype)


def per_device_split(
    features,
    grad_out,
    query_weight,
    key_weight,
    value_weight,
    out_weight,
    query_scale,
    key_scale,
    value_scale,
    out_scale,
    active_blocks,
    active_count,
):
    x, y, z, c = (lax.axis_index(a) for a in ("tm", "groups", "space", "rep"))
    width, tokens = features.shape
    mine = width // 2
    both = 2 * tokens
    slots = active_blocks.shape[1] * BLOCK
    scale = 1.0 / math.sqrt(HEAD_DIM * slots * lax.axis_size(REDUCE_AXES))
    pos = jnp.stack([z, c, x, y]).astype(jnp.int32)

    def own_scale(v):
        return lax.dynamic_index_in_dim(v.reshape(4, 2, 128), c, 1, keepdims=False).reshape(mine)

    half = query_weight.shape[0] // 2
    q_half, k_half, v_half, o_half = call(
        send_body,
        [shape((half, mine))] * 3 + [shape((half // 2, width))],
        [SMEM] + [ANY] * 4,
        (pos, query_weight, key_weight, value_weight, out_weight),
        (pltpu.SemaphoreType.DMA((13,)),),
        out_specs=(ANY,) * 4,
    )
    k = (key_weight,) + pieces(k_half, swap_x)
    v = (value_weight,) + pieces(v_half, swap_y)
    q = (query_weight,) + pieces(q_half, swap_x)
    o = (out_weight,) + pieces(o_half, swap_y)
    x_own, g_own = call(
        mask_body,
        [shape((tokens, width)), shape((width, tokens))],
        [SMEM, SMEM] + [VMEM] * 3,
        (active_blocks, active_count, features, grad_out, out_scale[:, None]),
        limit=24 << 20,
    )
    x_other, g_other = swap_core(x_own), swap_core(g_own)

    ks, vs, qs = own_scale(key_scale), own_scale(value_scale), own_scale(query_scale)
    sems = pltpu.SemaphoreType.DMA((22,))
    tall, wide = pltpu.VMEM((width, mine), BF16), pltpu.VMEM((mine, width), BF16)
    kept = pltpu.VMEM((both, mine), BF16)
    ff = 2 * both * width * mine
    key, value, state = call(
        key_value_body,
        [shape((both, mine)), shape((both, mine)), shape((256, 128), F32)],
        [SMEM] + [VMEM] * 4 + [ANY] * 14,
        (pos, x_own, x_other, ks[None], vs[None], *k, *v),
        (kept, kept, tall, tall, sems), 2 * ff, 24 << 20, (ANY, ANY, VMEM),
    )
    state = sum_over_chips(state)
    query, back, term = call(
        functools.partial(query_back_body, scale),
        [shape((both, mine)), shape((mine, both)), shape((256, 128), F32)],
        [SMEM] + [VMEM] * 5 + [ANY] * 14,
        (pos, x_own, x_other, g_own, g_other, qs[None], *q, *o),
        (tall, wide, sems), 2 * ff, 24 << 20,
    )
    term = sum_over_chips(term)
    diag = pltpu.VMEM((256, 256), BF16)
    out_own, out_other, in_own, in_other = call(
        functools.partial(middle_body, scale),
        [shape((tokens, width), F32), shape((tokens, width)),
         shape((width, tokens), F32), shape((width, tokens), F32)],
        [SMEM] + [VMEM] * 4 + [ANY] * 14,
        (pos, query, back, state, qs[:, None], *q, *o),
        (diag, kept, pltpu.VMEM((mine, both), BF16), tall, wide, sems), 2 * ff, 32 << 20,
    )
    out_sum = out_own + swap_core(out_other).astype(F32)
    attention_out = (out_sum * out_scale[None, :]).astype(BF16).T
    res_own, res_other = call(
        tail_body,
        [shape((width, tokens), F32), shape((width, tokens))],
        [SMEM] + [VMEM] * 7 + [ANY] * 14,
        (pos, key, value, term, ks[None], vs[None], in_own, in_other, *k, *v),
        (diag, kept, kept, tall, tall, sems), 2 * ff, 32 << 20,
    )
    input_grad = (res_own + swap_core(res_other).astype(F32)).astype(BF16)
    return attention_out, input_grad


highest = lax.Precision.HIGHEST
contract_first = (((0,), (0,)), ((), ()))


def compact_local(values, blocks, live_count):
    feature_rows = values.shape[0]
    block_grid = values.reshape(feature_rows, -1, BLOCK)
    picked = jnp.take(block_grid, blocks, axis=1)
    live_mask = (jnp.arange(blocks.shape[0], dtype=jnp.int32) < live_count).astype(values.dtype)
    return (picked * live_mask[None, :, None]).reshape(feature_rows, blocks.shape[0] * BLOCK)


def expand_local(values, blocks, total_blocks):
    feature_rows = values.shape[0]
    shaped = values.reshape(feature_rows, blocks.shape[0], BLOCK)
    target = jnp.zeros((feature_rows, total_blocks, BLOCK), values.dtype)
    return target.at[:, blocks, :].set(shaped).reshape(feature_rows, total_blocks * BLOCK)


def per_device_whole(
    features,
    grad_out,
    query_weight,
    key_weight,
    value_weight,
    out_weight,
    query_scale,
    key_scale,
    value_scale,
    out_scale,
    active_blocks,
    active_count,
):
    blocks = active_blocks[0]
    live_count = active_count[0]
    total_blocks = features.shape[1] // BLOCK
    slot_rows = blocks.shape[0] * BLOCK
    model_width = features.shape[0]
    attn_scale = 1.0 / math.sqrt(HEAD_DIM * slot_rows * lax.axis_size(("space", "tm", "rep")))
    scaled_grad = (grad_out.astype(jnp.float32) * out_scale[:, None]).astype(jnp.bfloat16)
    x_rows = compact_local(features, blocks, live_count)
    g_rows = compact_local(scaled_grad, blocks, live_count)
    pieces = (
        lax.all_gather(query_weight, "space", axis=0, tiled=True),
        lax.all_gather(key_weight, "space", axis=0, tiled=True),
        lax.all_gather(value_weight, "space", axis=0, tiled=True),
    )
    part_rows = x_rows
    q_raw, k_raw, v_raw = tuple(
        (
            lax.dot_general(piece_w, part_rows, contract_first, preferred_element_type=jnp.float32)
            for piece_w in pieces
        )
    )
    back_raw = jnp.dot(
        lax.all_gather(out_weight, "space", axis=0, tiled=True),
        g_rows,
        preferred_element_type=jnp.float32,
    )
    query = (q_raw * query_scale[:, None]).astype(jnp.bfloat16)
    key = (k_raw * key_scale[:, None]).astype(jnp.bfloat16)
    value = (v_raw * value_scale[:, None]).astype(jnp.bfloat16)
    back = back_raw.astype(jnp.bfloat16)
    q_heads = query.reshape(HEADS, HEAD_DIM, slot_rows)
    k_heads = key.reshape(HEADS, HEAD_DIM, slot_rows)
    v_heads = value.reshape(HEADS, HEAD_DIM, slot_rows)
    b_heads = back.reshape(HEADS, HEAD_DIM, slot_rows)
    state_local = jnp.einsum("hit,hjt->hij", k_heads, v_heads, preferred_element_type=jnp.float32)
    grad_local = attn_scale * jnp.einsum(
        "hit,hjt->hij", q_heads, b_heads, preferred_element_type=jnp.float32
    )
    state, state_grad = lax.psum((state_local, grad_local), ("space", "tm", "rep"))
    attended = attn_scale * jnp.einsum(
        "hij,hit->hjt", state, q_heads.astype(jnp.float32), precision=highest
    )
    attended = attended.astype(jnp.bfloat16).reshape(model_width, slot_rows)
    query_back = attn_scale * jnp.einsum(
        "hij,hjt->hit", state, b_heads.astype(jnp.float32), precision=highest
    )
    query_back = (query_back.reshape(model_width, slot_rows) * query_scale[:, None]).astype(
        jnp.bfloat16
    )
    key_back = jnp.einsum(
        "hij,hjt->hit", state_grad, v_heads.astype(jnp.float32), precision=highest
    )
    key_back = (key_back.reshape(model_width, slot_rows) * key_scale[:, None]).astype(jnp.bfloat16)
    value_back = jnp.einsum(
        "hij,hit->hjt", state_grad, k_heads.astype(jnp.float32), precision=highest
    )
    value_back = (value_back.reshape(model_width, slot_rows) * value_scale[:, None]).astype(
        jnp.bfloat16
    )
    part_rows = attended
    y_raw = lax.dot_general(
        lax.all_gather(out_weight, "space", axis=0, tiled=True),
        part_rows,
        contract_first,
        preferred_element_type=jnp.float32,
    )
    pieces = (
        lax.all_gather(query_weight, "space", axis=0, tiled=True),
        lax.all_gather(key_weight, "space", axis=0, tiled=True),
        lax.all_gather(value_weight, "space", axis=0, tiled=True),
    )
    new_rows = jnp.dot(pieces[0], query_back, preferred_element_type=jnp.float32)
    new_rows = new_rows + jnp.dot(pieces[1], key_back, preferred_element_type=jnp.float32)
    new_rows = new_rows + jnp.dot(pieces[2], value_back, preferred_element_type=jnp.float32)
    out_rows = (y_raw * out_scale[:, None]).astype(jnp.bfloat16)
    in_rows = new_rows.astype(jnp.bfloat16)
    return (
        expand_local(out_rows, blocks, total_blocks),
        expand_local(in_rows, blocks, total_blocks),
    )


def solution(mesh):
    fits = mesh.shape["space"] == 4 and all(
        mesh.shape[a] == 2 for a in ("groups", "tm", "rep")
    )
    split = P(None, DEVICE_AXES)
    placed = (
        split,
        split,
        P("space", None),
        P("space", None),
        P("space", None),
        P("space", None),
        P(),
        P(),
        P(),
        P(),
        P(DEVICE_AXES, None),
        P(DEVICE_AXES),
    )
    return jax.shard_map(
        per_device_split if fits else per_device_whole,
        mesh=mesh,
        in_specs=placed,
        out_specs=(split, split),
        check_vma=False,
    )
```

```python
import functools
import math

import jax
import jax.numpy as jnp
from jax import lax
from jax.experimental import pallas as pl
from jax.experimental.pallas import tpu as pltpu
from jax.sharding import PartitionSpec as P

HEADS = 16
HEAD_DIM = 64
BLOCK = 64
BF16 = jnp.bfloat16
F32 = jnp.float32
REDUCE_AXES = ("space", "tm", "rep")
DEVICE_AXES = ("groups", "space", "tm", "rep")

VMEM = pl.BlockSpec(memory_space=pltpu.VMEM)
ANY = pl.BlockSpec(memory_space=pl.ANY)
SMEM = pl.BlockSpec(memory_space=pltpu.SMEM)


def dot(a, b, ca, cb):
    return lax.dot_general(a, b, (((ca,), (cb,)), ((), ())), preferred_element_type=F32)


def call(body, outs, in_specs, args, scratch=(), flops=0, limit=None, out_specs=None):
    size = sum(math.prod(o.shape) * o.dtype.itemsize for o in outs)
    size += sum(math.prod(a.shape) * a.dtype.itemsize for a in args)
    return pl.pallas_call(
        body,
        out_shape=tuple(outs),
        in_specs=in_specs,
        out_specs=out_specs or (VMEM,) * len(outs),
        scratch_shapes=scratch,
        compiler_params=pltpu.CompilerParams(vmem_limit_bytes=limit),
        cost_estimate=pl.CostEstimate(flops=flops, bytes_accessed=size, transcendentals=0),
    )(*args)


def shape(dims, dtype=BF16):
    return jax.ShapeDtypeStruct(dims, dtype)


def swap_x(a):
    return lax.ppermute(a, "tm", [(0, 1), (1, 0)])


def swap_y(a):
    return lax.ppermute(a, "groups", [(0, 1), (1, 0)])


def swap_core(a):
    return lax.ppermute(a, "rep", [(0, 1), (1, 0)])


def turn_z(a, step):
    return lax.ppermute(a, "space", [(i, (i + step) % 4) for i in range(4)])


def pieces(quarter, first, second):
    near = tuple(turn_z(quarter, step) for step in (1, 3, 2))
    side = tuple(first(a) for a in near)
    return near + side + tuple(second(a) for a in near) + tuple(second(a) for a in side)


def sum_over_chips(part):
    part = part + swap_x(part.astype(BF16)).astype(F32)
    sent = part.astype(BF16)
    for step in (1, 3, 2):
        part = part + turn_z(sent, step).astype(F32)
    return part


def aligned(index, size):
    return pl.ds(pl.multiple_of(index * size, size), size)


def send_body(pos, q, k, v, o, kv, qo, sems):
    c, part = pos[1], pos[2]
    copies = []

    def add(src, dst):
        copies.append(pltpu.make_async_copy(src, dst, sems.at[len(copies)]))

    for ref, out, base in ((k, kv, 0), (v, kv, 64), (q, qo, 0)):
        for j in range(4):
            cols = pl.ds(pl.multiple_of(256 * j + 128 * c, 128), 128)
            dst = out.at[base : base + 64, 128 * j : 128 * j + 128]
            add(ref.at[aligned(part, 64), cols], dst)
    for n in range(2):
        src = o.at[aligned(4 * c + part, 32), 512 * n : 512 * n + 512]
        add(src, qo.at[64 + 32 * n : 96 + 32 * n])
    for one in copies:
        one.start()
    for one in copies:
        one.wait()


def mask_body(blocks, count, features, grad, scale, rows, cols):
    tokens = features.shape[1]
    block_of = lax.broadcasted_iota(jnp.int32, (1, tokens), 1) // BLOCK
    mask = jnp.zeros((1, tokens), F32)
    for j in range(blocks.shape[1]):
        named = jnp.where(j < count[0], blocks[0, j], -1)
        mask = jnp.where(block_of == named, 1.0, mask)
    for t in range(0, features.shape[0], 256):
        at = slice(t, t + 256)
        rows[:, at] = (features[at, :].astype(F32) * mask).astype(BF16).T
        cols[at, :] = (grad[at, :].astype(F32) * scale[at, :] * mask).astype(BF16)


def place(pos_ref, own_ref, parts, full_ref, sems, flips, base, begin, by_rows=False):
    z, c, part = pos_ref[0], pos_ref[1], pos_ref[2]
    copies = []

    def add(src, dst):
        copies.append(pltpu.make_async_copy(src, dst, sems.at[base + len(copies)]))

    if by_rows:
        add(own_ref.at[aligned(c, 128)], full_ref.at[aligned(z, 128)])
    else:
        for j in range(4):
            cols = pl.ds(pl.multiple_of(256 * j + 128 * c, 128), 128)
            add(own_ref.at[:, cols], full_ref.at[aligned(z, 256), 128 * j : 128 * j + 128])
    for n, ref in enumerate(parts):
        flip = (0,) + flips + (3,)
        at = lax.rem(z + (3, 1, 2)[n % 3], 4) * 4 + lax.bitwise_xor(part, flip[n // 3])
        if by_rows:
            for m in range(2):
                dst = full_ref.at[aligned(at, 32), 512 * m : 512 * m + 512]
                add(ref.at[begin + 32 * m : begin + 32 * m + 32], dst)
        else:
            add(ref.at[begin : begin + 64], full_ref.at[aligned(at, 64)])
    for one in copies:
        one.start()
    return copies


def wait(copies):
    for one in copies:
        one.wait()


def pack(block):
    left = lax.broadcasted_iota(jnp.int32, (HEAD_DIM, 128), 1) < HEAD_DIM
    return (
        jnp.where(left, block[0:64, 0:128], block[64:128, 0:128]),
        jnp.where(left, block[128:192, 128:256], block[192:256, 128:256]),
    )


def unpack(packed, full_ref):
    left = lax.broadcasted_iota(jnp.int32, (HEAD_DIM, 128), 1) < HEAD_DIM
    full_ref[...] = jnp.zeros_like(full_ref)
    for n in range(2):
        two = packed[64 * n : 64 * n + 64]
        full_ref[128 * n : 128 * n + 64, 128 * n : 128 * n + 128] = jnp.where(
            left, two, 0.0
        ).astype(full_ref.dtype)
        full_ref[128 * n + 64 : 128 * n + 128, 128 * n : 128 * n + 128] = jnp.where(
            left, 0.0, two
        ).astype(full_ref.dtype)


def key_value_body(pos, x_own, x_other, ks, vs, *refs):
    k, v, parts = refs[0], refs[1], refs[2:14]
    key_out, value_out, state, key, value, wk, wv, sems = refs[14:]
    fetch_k = place(pos, k, parts, wk, sems, (1, 2), 0, 0)
    fetch_v = place(pos, v, parts, wv, sems, (1, 2), 16, 64)
    half = x_own.shape[0]
    stores = []
    for fetch, w, scale, dst, out in (
        (fetch_k, wk, ks, key, key_out), (fetch_v, wv, vs, value, value_out)
    ):
        wait(fetch)
        for n, rows in enumerate((x_own, x_other)):
            for t in range(0, half, 256):
                at = slice(n * half + t, n * half + t + 256)
                dst[at, :] = (dot(rows[t : t + 256, :], w[...], 1, 0) * scale[...]).astype(BF16)
        stores.append(pltpu.make_async_copy(dst, out, sems.at[41 + len(stores)]))
        stores[-1].start()
    for g in range(2):
        cols = slice(256 * g, 256 * g + 256)
        a, b = pack(dot(key[:, cols], value[:, cols], 0, 0))
        state[128 * g : 128 * g + 64, :] = a
        state[128 * g + 64 : 128 * g + 128, :] = b
    wait(stores)


def query_back_body(scale, pos, x_own, x_other, g_own, g_other, qs, *refs):
    q, o, parts = refs[0], refs[1], refs[2:14]
    query, back, term, wq, wo, sems = refs[14:]
    fetch_q = place(pos, q, parts, wq, sems, (2, 1), 0, 0)
    fetch_o = place(pos, o, parts, wo, sems, (2, 1), 16, 64, True)
    half = x_own.shape[0]
    wait(fetch_q)
    for n, rows in enumerate((x_own, x_other)):
        for t in range(0, half, 256):
            at = slice(n * half + t, n * half + t + 256)
            query[at, :] = (dot(rows[t : t + 256, :], wq[...], 1, 0) * qs[...]).astype(BF16)
    wait(fetch_o)
    for n, cols in enumerate((g_own, g_other)):
        for t in range(0, half, 256):
            at = slice(n * half + t, n * half + t + 256)
            back[:, at] = dot(wo[...], cols[:, t : t + 256], 1, 0).astype(BF16)
    for g in range(2):
        part = slice(256 * g, 256 * g + 256)
        a, b = pack(scale * dot(back[part, :], query[:, part], 1, 0))
        term[128 * g : 128 * g + 64, :] = a
        term[128 * g + 64 : 128 * g + 128, :] = b


def middle_body(scale, pos, query, back, state, qs, *refs):
    q, o, parts = refs[0], refs[1], refs[2:14]
    out_own, out_other, in_own, in_other, diag, att, qb, wq, wo, sems = refs[14:]
    fetch_o = place(pos, o, parts, wo, sems, (2, 1), 16, 64, True)
    fetch_q = place(pos, q, parts, wq, sems, (2, 1), 0, 0)
    half = out_own.shape[0]
    for g in range(2):
        part = slice(256 * g, 256 * g + 256)
        unpack(scale * state[128 * g : 128 * g + 128, :], diag)
        att[:, part] = dot(query[:, part], diag[...], 1, 0).astype(BF16)
        qb[part, :] = (dot(diag[...], back[part, :], 1, 0) * qs[part, :]).astype(BF16)
    wait(fetch_o)
    wait(fetch_q)
    for n, (out, inp) in enumerate(((out_own, in_own), (out_other, in_other))):
        for t in range(0, half, 256):
            at = slice(n * half + t, n * half + t + 256)
            out[t : t + 256, :] = dot(att[at, :], wo[...], 1, 0).astype(out.dtype)
            inp[:, t : t + 256] = dot(wq[...], qb[:, at], 1, 0)


def tail_body(pos, key, value, term, ks, vs, in_own, in_other, *refs):
    k, v, parts = refs[0], refs[1], refs[2:14]
    res_own, res_other, diag, kb, vb, wk, wv, sems = refs[14:]
    fetch = place(pos, k, parts, wk, sems, (1, 2), 0, 0)
    fetch += place(pos, v, parts, wv, sems, (1, 2), 16, 64)
    half = in_own.shape[1]
    for g in range(2):
        part = slice(256 * g, 256 * g + 256)
        unpack(term[128 * g : 128 * g + 128, :], diag)
        kb[:, part] = (dot(value[:, part], diag[...], 1, 0) * ks[:, part]).astype(BF16)
        vb[:, part] = (dot(key[:, part], diag[...], 1, 1) * vs[:, part]).astype(BF16)
    wait(fetch)
    for n, (inp, res) in enumerate(((in_own, res_own), (in_other, res_other))):
        for t in range(0, half, 256):
            at = slice(n * half + t, n * half + t + 256)
            total = inp[:, t : t + 256] + dot(wk[...], kb[at, :], 1, 1)
            total = total + dot(wv[...], vb[at, :], 1, 1)
            res[:, t : t + 256] = total.astype(res.dtype)


def per_device_split(
    features,
    grad_out,
    query_weight,
    key_weight,
    value_weight,
    out_weight,
    query_scale,
    key_scale,
    value_scale,
    out_scale,
    active_blocks,
    active_count,
):
    x, y, z, c = (lax.axis_index(a) for a in ("tm", "groups", "space", "rep"))
    width, tokens = features.shape
    mine = width // 2
    both = 2 * tokens
    slots = active_blocks.shape[1] * BLOCK
    scale = 1.0 / math.sqrt(HEAD_DIM * slots * lax.axis_size(REDUCE_AXES))
    pos = jnp.stack([z, c, 2 * y + x]).astype(jnp.int32)

    def own_scale(v):
        return lax.dynamic_index_in_dim(v.reshape(4, 2, 128), c, 1, keepdims=False).reshape(mine)

    kv, qo = call(
        send_body,
        [shape((128, mine))] * 2,
        [SMEM] + [ANY] * 4,
        (pos, query_weight, key_weight, value_weight, out_weight),
        (pltpu.SemaphoreType.DMA((14,)),),
    )
    kv = (key_weight, value_weight) + pieces(kv, swap_x, swap_y)
    qo = (query_weight, out_weight) + pieces(qo, swap_y, swap_x)
    x_own, g_own = call(
        mask_body,
        [shape((tokens, width)), shape((width, tokens))],
        [SMEM, SMEM] + [VMEM] * 3,
        (active_blocks, active_count, features, grad_out, out_scale[:, None]),
        limit=24 << 20,
    )
    x_other, g_other = swap_core(x_own), swap_core(g_own)

    ks, vs, qs = own_scale(key_scale), own_scale(value_scale), own_scale(query_scale)
    sems = pltpu.SemaphoreType.DMA((43,))
    tall, wide = pltpu.VMEM((width, mine), BF16), pltpu.VMEM((mine, width), BF16)
    kept = pltpu.VMEM((both, mine), BF16)
    ff = 2 * both * width * mine
    key, value, state = call(
        key_value_body,
        [shape((both, mine)), shape((both, mine)), shape((256, 128), F32)],
        [SMEM] + [VMEM] * 4 + [ANY] * 14,
        (pos, x_own, x_other, ks[None], vs[None], *kv),
        (kept, kept, tall, tall, sems), 2 * ff, 24 << 20, (ANY, ANY, VMEM),
    )
    state = sum_over_chips(state)
    query, back, term = call(
        functools.partial(query_back_body, scale),
        [shape((both, mine)), shape((mine, both)), shape((256, 128), F32)],
        [SMEM] + [VMEM] * 5 + [ANY] * 14,
        (pos, x_own, x_other, g_own, g_other, qs[None], *qo),
        (tall, wide, sems), 2 * ff, 24 << 20,
    )
    term = sum_over_chips(term)
    diag = pltpu.VMEM((256, 256), BF16)
    out_own, out_other, in_own, in_other = call(
        functools.partial(middle_body, scale),
        [shape((tokens, width), F32), shape((tokens, width)),
         shape((width, tokens), F32), shape((width, tokens), F32)],
        [SMEM] + [VMEM] * 4 + [ANY] * 14,
        (pos, query, back, state, qs[:, None], *qo),
        (diag, kept, pltpu.VMEM((mine, both), BF16), tall, wide, sems), 2 * ff, 32 << 20,
    )
    out_sum = out_own + swap_core(out_other).astype(F32)
    attention_out = (out_sum * out_scale[None, :]).astype(BF16).T
    res_own, res_other = call(
        tail_body,
        [shape((width, tokens), F32), shape((width, tokens))],
        [SMEM] + [VMEM] * 7 + [ANY] * 14,
        (pos, key, value, term, ks[None], vs[None], in_own, in_other, *kv),
        (diag, kept, kept, tall, tall, sems), 2 * ff, 32 << 20,
    )
    input_grad = (res_own + swap_core(res_other).astype(F32)).astype(BF16)
    return attention_out, input_grad


highest = lax.Precision.HIGHEST
contract_first = (((0,), (0,)), ((), ()))


def compact_local(values, blocks, live_count):
    feature_rows = values.shape[0]
    block_grid = values.reshape(feature_rows, -1, BLOCK)
    picked = jnp.take(block_grid, blocks, axis=1)
    live_mask = (jnp.arange(blocks.shape[0], dtype=jnp.int32) < live_count).astype(values.dtype)
    return (picked * live_mask[None, :, None]).reshape(feature_rows, blocks.shape[0] * BLOCK)


def expand_local(values, blocks, total_blocks):
    feature_rows = values.shape[0]
    shaped = values.reshape(feature_rows, blocks.shape[0], BLOCK)
    target = jnp.zeros((feature_rows, total_blocks, BLOCK), values.dtype)
    return target.at[:, blocks, :].set(shaped).reshape(feature_rows, total_blocks * BLOCK)


def per_device_whole(
    features,
    grad_out,
    query_weight,
    key_weight,
    value_weight,
    out_weight,
    query_scale,
    key_scale,
    value_scale,
    out_scale,
    active_blocks,
    active_count,
):
    blocks = active_blocks[0]
    live_count = active_count[0]
    total_blocks = features.shape[1] // BLOCK
    slot_rows = blocks.shape[0] * BLOCK
    model_width = features.shape[0]
    attn_scale = 1.0 / math.sqrt(HEAD_DIM * slot_rows * lax.axis_size(("space", "tm", "rep")))
    scaled_grad = (grad_out.astype(jnp.float32) * out_scale[:, None]).astype(jnp.bfloat16)
    x_rows = compact_local(features, blocks, live_count)
    g_rows = compact_local(scaled_grad, blocks, live_count)
    pieces = (
        lax.all_gather(query_weight, "space", axis=0, tiled=True),
        lax.all_gather(key_weight, "space", axis=0, tiled=True),
        lax.all_gather(value_weight, "space", axis=0, tiled=True),
    )
    part_rows = x_rows
    q_raw, k_raw, v_raw = tuple(
        (
            lax.dot_general(piece_w, part_rows, contract_first, preferred_element_type=jnp.float32)
            for piece_w in pieces
        )
    )
    back_raw = jnp.dot(
        lax.all_gather(out_weight, "space", axis=0, tiled=True),
        g_rows,
        preferred_element_type=jnp.float32,
    )
    query = (q_raw * query_scale[:, None]).astype(jnp.bfloat16)
    key = (k_raw * key_scale[:, None]).astype(jnp.bfloat16)
    value = (v_raw * value_scale[:, None]).astype(jnp.bfloat16)
    back = back_raw.astype(jnp.bfloat16)
    q_heads = query.reshape(HEADS, HEAD_DIM, slot_rows)
    k_heads = key.reshape(HEADS, HEAD_DIM, slot_rows)
    v_heads = value.reshape(HEADS, HEAD_DIM, slot_rows)
    b_heads = back.reshape(HEADS, HEAD_DIM, slot_rows)
    state_local = jnp.einsum("hit,hjt->hij", k_heads, v_heads, preferred_element_type=jnp.float32)
    grad_local = attn_scale * jnp.einsum(
        "hit,hjt->hij", q_heads, b_heads, preferred_element_type=jnp.float32
    )
    state, state_grad = lax.psum((state_local, grad_local), ("space", "tm", "rep"))
    attended = attn_scale * jnp.einsum(
        "hij,hit->hjt", state, q_heads.astype(jnp.float32), precision=highest
    )
    attended = attended.astype(jnp.bfloat16).reshape(model_width, slot_rows)
    query_back = attn_scale * jnp.einsum(
        "hij,hjt->hit", state, b_heads.astype(jnp.float32), precision=highest
    )
    query_back = (query_back.reshape(model_width, slot_rows) * query_scale[:, None]).astype(
        jnp.bfloat16
    )
    key_back = jnp.einsum(
        "hij,hjt->hit", state_grad, v_heads.astype(jnp.float32), precision=highest
    )
    key_back = (key_back.reshape(model_width, slot_rows) * key_scale[:, None]).astype(jnp.bfloat16)
    value_back = jnp.einsum(
        "hij,hit->hjt", state_grad, k_heads.astype(jnp.float32), precision=highest
    )
    value_back = (value_back.reshape(model_width, slot_rows) * value_scale[:, None]).astype(
        jnp.bfloat16
    )
    part_rows = attended
    y_raw = lax.dot_general(
        lax.all_gather(out_weight, "space", axis=0, tiled=True),
        part_rows,
        contract_first,
        preferred_element_type=jnp.float32,
    )
    pieces = (
        lax.all_gather(query_weight, "space", axis=0, tiled=True),
        lax.all_gather(key_weight, "space", axis=0, tiled=True),
        lax.all_gather(value_weight, "space", axis=0, tiled=True),
    )
    new_rows = jnp.dot(pieces[0], query_back, preferred_element_type=jnp.float32)
    new_rows = new_rows + jnp.dot(pieces[1], key_back, preferred_element_type=jnp.float32)
    new_rows = new_rows + jnp.dot(pieces[2], value_back, preferred_element_type=jnp.float32)
    out_rows = (y_raw * out_scale[:, None]).astype(jnp.bfloat16)
    in_rows = new_rows.astype(jnp.bfloat16)
    return (
        expand_local(out_rows, blocks, total_blocks),
        expand_local(in_rows, blocks, total_blocks),
    )


def solution(mesh):
    fits = mesh.shape["space"] == 4 and all(
        mesh.shape[a] == 2 for a in ("groups", "tm", "rep")
    )
    split = P(None, DEVICE_AXES)
    placed = (
        split,
        split,
        P("space", None),
        P("space", None),
        P("space", None),
        P("space", None),
        P(),
        P(),
        P(),
        P(),
        P(DEVICE_AXES, None),
        P(DEVICE_AXES),
    )
    return jax.shard_map(
        per_device_split if fits else per_device_whole,
        mesh=mesh,
        in_specs=placed,
        out_specs=(split, split),
        check_vma=False,
    )
```
